512 devices in a mesh: dp: 512 (over x, y, z, core).
Axes of the slice: x: 4, y: 4, z: 16, core: 2. Of those that a mesh axis runs over, the one named last changes fastest.
Arguments:
- images: bfloat16 [2, 512, 784, 512], P(None, 'dp'), may hold values from -6 to 6
- cotangent: bfloat16 [2, 512, 784, 512], P(None, 'dp'), may hold values from -0.23925781 to 0.23925781
- w_reduce: float32 [512, 65536], P('dp'), may hold values from -1 to 1
- w_spatial: float32 [512, 147456], P('dp'), may hold values from -0.75 to 0.75
- w_expand: float32 [512, 65536], P('dp'), may hold values from -2 to 2
- norm_gain: float32 [512, 768], P('dp'), may hold values from 0.5 to 1.5
- norm_bias: float32 [512, 768], P('dp'), may hold values from -1.2 to 1.2
- round_index: int32 [1], replicated, may hold values from 0 to 63
Outputs:
- avg_reduce: float32 [65536], P('dp')
- avg_spatial: float32 [147456], P('dp')
- avg_expand: float32 [65536], P('dp')
- avg_norm: float32 [1536], P('dp')
- moment_reduce: bfloat16 [512, 65536], P('dp')
- moment_spatial: bfloat16 [512, 147456], P('dp')
- moment_expand: bfloat16 [512, 65536], P('dp')
- moment_norm: bfloat16 [512, 1536], P('dp')
The draws below stay inside these ranges and needn't reach their ends.
All inputs are finite; a program needn't handle non-finite values.
Results may differ from the reference program's by a relative error of at most 0.017.
Values sent between devices are 32-bit elements; how exact they have to be, the bound alone decides.
A program may use at most 64 MiB of HBM per device.

```python
import jax
import jax.numpy as jnp
from jax import lax

C_IN = 512
C_MID = 128
HEIGHT = 28
WIDTH = 28
KSIZE = 3
STEPS = 2
IMG_DEV = 1
PIXELS = 784
REPLICAS = 512
IMAGES = 512
NORM_CH = 768
N_DP = 512


def raised(values, key, source, target, blocks, factor):
    owner, partner = [(jnp.arange(values.shape[dim]) // (values.shape[dim] // blocks)).reshape([-1 if axis == dim else 1 for axis in range(values.ndim)]) for dim in (source, target)]
    chosen = jax.random.permutation(key, blocks)[partner]
    strong = (owner == chosen) | (owner == (partner + blocks // 2) % blocks)
    return jnp.where(strong, factor * values, values)


def shard_levels(key, extent, shards, low, high):
    factor_of, own = 1.0, jax.random.fold_in(key, 6)
    for axis_at, shards_of in shards:
        heights = jnp.exp(jax.random.uniform(jax.random.fold_in(own, axis_at), (shards_of,), jnp.float32, low / len(shards), high / len(shards)))
        factor_of = factor_of * jnp.repeat(heights, extent[axis_at] // shards_of).reshape([-1 if axis == axis_at else 1 for axis in range(len(extent))])
    return factor_of


def centred(rng, shape, spread, most, shards=(), kind=jnp.bfloat16):
    array = spread * jax.random.normal(rng, shape, jnp.float32)
    if shards:
        array = array * shard_levels(rng, shape, shards, -0.22, 0.18)
    return jnp.clip(array, -most, most).astype(kind)


def heavy_noise(own_key, shape, scale, reach, shards, heavy, kind=jnp.bfloat16):
    values = scale * jax.random.normal(own_key, shape, jnp.float32)
    if shards:
        values = values * shard_levels(own_key, shape, shards, -0.22, 0.18)
    return jnp.clip(raised(values, jax.random.fold_in(own_key, 3), *heavy), -reach, reach).astype(kind)


def setup_inputs(seed: int = 0) -> dict:
    arg_keys = jax.random.split(jax.random.key(seed), 9)
    images = centred(arg_keys[0], (STEPS, IMAGES, PIXELS, C_IN), 1.0, 6.0, ((1, 512),))
    cotangent = centred(arg_keys[1], (STEPS, IMAGES, PIXELS, C_IN), 0.04, 0.23925781, ((1, 512),))
    w_reduce = heavy_noise(arg_keys[2], (REPLICAS, C_IN * C_MID), C_IN ** -0.5, 1.0, ((0, 512),), (0, 1, 512, 6.0), jnp.float32)
    w_spatial = heavy_noise(arg_keys[3], (REPLICAS, KSIZE * KSIZE * C_MID * C_MID), (KSIZE * KSIZE * C_MID) ** -0.5, 0.75, ((0, 512),), (0, 1, 512, 6.0), jnp.float32)
    w_expand = heavy_noise(arg_keys[4], (REPLICAS, C_MID * C_IN), C_MID ** -0.5, 2.0, ((0, 512),), (0, 1, 512, 6.0), jnp.float32)
    norm_gain = jnp.clip(1.0 + 0.1 * jax.random.normal(arg_keys[5], (REPLICAS, NORM_CH), jnp.float32), 0.5, 1.5)
    norm_bias = centred(arg_keys[6], (REPLICAS, NORM_CH), 0.3, 1.2, ((0, 512),), jnp.float32)
    round_index = jax.random.randint(arg_keys[7], (1,), 0, 64).astype(jnp.int32)
    return dict(images=images, cotangent=cotangent, w_reduce=w_reduce, w_spatial=w_spatial, w_expand=w_expand, norm_gain=norm_gain, norm_bias=norm_bias, round_index=round_index)


LEARN_RATE = 0.01
MOMENTUM = 0.9
EPSILON = 1e-05

def contract_rows(left, right):
    return lax.dot_general(left, right, (((0,), (0,)), ((), ())), preferred_element_type=jnp.float32)

def contract_cols(left, right):
    return lax.dot_general(left, right, (((1,), (1,)), ((), ())), preferred_element_type=jnp.float32)

def activate(values):
    return values * jax.nn.sigmoid(values)

def act_slope(values):
    sigma = jax.nn.sigmoid(values)
    return sigma * (1.0 + values * (1.0 - sigma))

def patches(source):
    channels = source.shape[1]
    margin = KSIZE // 2
    grid_view = source.reshape(-1, HEIGHT, WIDTH, channels)
    padded = jnp.pad(grid_view, ((0, 0), (margin, margin), (margin, margin), (0, 0)))
    pieces = [padded[:, row_off:row_off + HEIGHT, col_off:col_off + WIDTH, :] for row_off in range(KSIZE) for col_off in range(KSIZE)]
    return jnp.concatenate(pieces, axis=3).reshape(-1, KSIZE * KSIZE * channels)

def normalize(values, gains, shifts):
    center = values - lax.optimization_barrier(jnp.mean(values, axis=0))
    inv_scale = lax.rsqrt(lax.optimization_barrier(jnp.mean(center * center, axis=0)) + EPSILON)
    normed = center * inv_scale
    return (normed, inv_scale, normed * gains + shifts)

def normalize_back(grad_out, normed, inv_scale, gains):
    grad_gain = lax.optimization_barrier(jnp.sum(grad_out * normed, axis=0))
    grad_shift = lax.optimization_barrier(jnp.sum(grad_out, axis=0))
    grad_normed = grad_out * gains
    grad_in = (grad_normed - lax.optimization_barrier(jnp.mean(grad_normed, axis=0)) - normed * lax.optimization_barrier(jnp.mean(grad_normed * normed, axis=0))) * inv_scale
    return (grad_in, grad_gain, grad_shift)

def replica_grads(pixels_in, upstream, reduce_flat, spatial_flat, expand_flat, gain_all, shift_all):
    in_ch = pixels_in.shape[1]
    mid_ch = reduce_flat.shape[0] // in_ch
    taps = KSIZE * KSIZE
    reduce_w = reduce_flat.reshape(in_ch, mid_ch).astype(jnp.bfloat16)
    spatial_w = spatial_flat.reshape(taps * mid_ch, mid_ch).astype(jnp.bfloat16)
    expand_w = expand_flat.reshape(mid_ch, in_ch).astype(jnp.bfloat16)
    gain_a, gain_b, gain_c = (gain_all[:mid_ch], gain_all[mid_ch:2 * mid_ch], gain_all[2 * mid_ch:])
    shift_a, shift_b, shift_c = (shift_all[:mid_ch], shift_all[mid_ch:2 * mid_ch], shift_all[2 * mid_ch:])
    first = jnp.dot(pixels_in, reduce_w, preferred_element_type=jnp.float32)
    normed_a, scale_a, out_a = normalize(first, gain_a, shift_a)
    hidden_a = activate(out_a).astype(jnp.bfloat16)
    patch_a = patches(hidden_a)
    second = jnp.dot(patch_a, spatial_w, preferred_element_type=jnp.float32)
    normed_b, scale_b, out_b = normalize(second, gain_b, shift_b)
    hidden_b = activate(out_b).astype(jnp.bfloat16)
    third = jnp.dot(hidden_b, expand_w, preferred_element_type=jnp.float32)
    normed_c, scale_c, out_c = normalize(third, gain_c, shift_c)
    summed = out_c + pixels_in.astype(jnp.float32)
    grad_sum = upstream.astype(jnp.float32) * act_slope(summed)
    grad_third, dgain_c, dshift_c = normalize_back(grad_sum, normed_c, scale_c, gain_c)
    grad_third = grad_third.astype(jnp.bfloat16)
    grad_expand = contract_rows(hidden_b, grad_third)
    grad_hidden_b = contract_cols(grad_third, expand_w)
    grad_out_b = grad_hidden_b * act_slope(out_b)
    grad_second, dgain_b, dshift_b = normalize_back(grad_out_b, normed_b, scale_b, gain_b)
    grad_second = grad_second.astype(jnp.bfloat16)
    grad_spatial = contract_rows(patch_a, grad_second)
    flipped = spatial_w.reshape(taps, mid_ch, mid_ch)[::-1].transpose(0, 2, 1).reshape(taps * mid_ch, mid_ch)
    grad_hidden_a = jnp.dot(patches(grad_second), flipped, preferred_element_type=jnp.float32)
    grad_out_a = grad_hidden_a * act_slope(out_a)
    grad_first, dgain_a, dshift_a = normalize_back(grad_out_a, normed_a, scale_a, gain_a)
    grad_reduce = contract_rows(pixels_in, grad_first.astype(jnp.bfloat16))
    return (grad_reduce.reshape(-1), grad_spatial.reshape(-1), grad_expand.reshape(-1), jnp.concatenate([dgain_a, dgain_b, dgain_c]), jnp.concatenate([dshift_a, dshift_b, dshift_c]))

def reference(images, cotangent, w_reduce, w_spatial, w_expand, norm_gain, norm_bias, round_index):
    levels = N_DP.bit_length() - 1
    replicas = jnp.arange(N_DP, dtype=jnp.int32)
    params = (w_reduce, w_spatial, w_expand, norm_gain, norm_bias)
    moments = tuple((jnp.zeros_like(member) for member in params))
    for step_index in range(STEPS):
        bit_now = ((round_index[0] + step_index) % levels).astype(jnp.int32)
        partner = jnp.bitwise_xor(replicas, jnp.left_shift(jnp.int32(1), bit_now)).astype(jnp.int32)
        blended = tuple(((member + jnp.take(member, partner, axis=0)) * 0.5 for member in params))
        batch_rows = images[step_index].reshape(N_DP, IMG_DEV * PIXELS, C_IN)
        target = cotangent[step_index].reshape(N_DP, IMG_DEV * PIXELS, C_IN)
        gradients = lax.map(lambda packed: replica_grads(*packed), (batch_rows, target) + blended)
        moments = tuple((MOMENTUM * held + newest for held, newest in zip(moments, gradients)))
        params = tuple((member - LEARN_RATE * held for member, held in zip(blended, moments)))
    averaged = tuple((lax.optimization_barrier(jnp.sum(member, axis=0)) / N_DP for member in params))
    avg_norm = jnp.concatenate([averaged[3], averaged[4]])
    moment_norm = jnp.concatenate([moments[3], moments[4]], axis=1)
    return (averaged[0], averaged[1], averaged[2], avg_norm, moments[0].astype(jnp.bfloat16), moments[1].astype(jnp.bfloat16), moments[2].astype(jnp.bfloat16), moment_norm.astype(jnp.bfloat16))
```

```python
import functools

import jax
import jax.numpy as jnp
from jax import lax
from jax.experimental import pallas as pl
from jax.experimental.pallas import tpu as pltpu
from jax.sharding import PartitionSpec as P

LEARN_RATE = 0.01
MOMENTUM = 0.9
EPSILON = 1e-05

C_IN = 512
C_MID = 128
WIDTH = 28
PIXELS = 784
ROWS = 112
CHUNKS = PIXELS // ROWS
ROWS_C = 16
CHUNKS_C = PIXELS // ROWS_C
PAD = 32
LANES = 128
REPLICAS = 512
LEVELS = 9

F32 = jnp.float32
BF16 = jnp.bfloat16
MESH = pl.DeviceIdType.MESH
VMEM = pl.BlockSpec(memory_space=pltpu.VMEM)
WEIGHTS = ((512, LANES), (1152, LANES), (512, LANES))
PARAMS = WEIGHTS + ((1, 768), (1, 768))


def shaped(shapes, dtype):
    return tuple(jax.ShapeDtypeStruct(shape, dtype) for shape in shapes)


def gossip_kernel(bit, *refs):
    count = len(PARAMS)
    own, mixed, theirs = refs[:count], refs[count : 2 * count], refs[2 * count : 3 * count]
    send_sem, recv_sem = refs[3 * count :]
    me = lax.axis_index("dp")
    step = 1 << bit
    partner = me + step - 2 * step * lax.rem(lax.div(me, step), 2)
    barrier = pltpu.get_barrier_semaphore()
    pl.semaphore_signal(barrier, inc=1, device_id=(partner,), device_id_type=MESH)
    pl.semaphore_wait(barrier, 1)
    copies = []
    for k in range(count):
        copy = pltpu.make_async_remote_copy(
            src_ref=own[k],
            dst_ref=theirs[k],
            send_sem=send_sem.at[k],
            recv_sem=recv_sem.at[k],
            device_id=(partner,),
            device_id_type=MESH,
        )
        copy.start()
        copies.append(copy)
    for k in range(count):
        copies[k].wait_recv()
        mixed[k][...] = (own[k][...] + theirs[k][...]) * 0.5
    for copy in copies:
        copy.wait_send()


def gossip(bit, *params):
    return pl.pallas_call(
        functools.partial(gossip_kernel, bit),
        out_shape=shaped(PARAMS, F32),
        in_specs=[VMEM] * 5,
        out_specs=(VMEM,) * 5,
        scratch_shapes=[pltpu.VMEM(shape, F32) for shape in PARAMS]
        + [pltpu.SemaphoreType.DMA((5,)), pltpu.SemaphoreType.DMA((5,))],
        compiler_params=pltpu.CompilerParams(collective_id=bit, has_side_effects=True),
        name=f"gossip{bit}",
    )(*params)


def mix(bit_choice, params):
    branches = [functools.partial(gossip, bit) for bit in range(LEVELS)]
    return lax.switch(bit_choice, branches, *params)


def contract(left, right, dims):
    return lax.dot_general(left, right, ((dims[0], dims[1]), ((), ())), preferred_element_type=F32)


def rows_sum(values):
    return jnp.sum(values.reshape(-1, 8, values.shape[-1]), axis=0)


def total(partial):
    return jnp.sum(partial, axis=0, keepdims=True)


def sigmoid(values):
    return 0.5 + 0.5 * jnp.tanh(0.5 * values)


def chunked(rows, chunks, body, init, unroll=1):
    def step(index, carry):
        return body(pl.ds(pl.multiple_of(index * rows, rows), rows), index * rows, carry)

    return lax.fori_loop(0, chunks, step, init, unroll=unroll)


def mean_and_scale(source, rows, chunks, width):
    zero = jnp.zeros((8, width), F32)
    mean = total(chunked(rows, chunks, lambda at, _, acc: acc + rows_sum(source[at, :]), zero)) * (1.0 / PIXELS)

    def spread(at, _, acc):
        center = source[at, :] - mean
        return acc + rows_sum(center * center)

    scale = lax.rsqrt(total(chunked(rows, chunks, spread, zero)) * (1.0 / PIXELS) + EPSILON)
    return mean, scale


def step_kernel(last, *refs):
    take = iter(refs)
    x_ref, cot_ref = next(take), next(take)
    mixed = [next(take) for _ in range(5)]
    held = [next(take) for _ in range(5)] if last else None
    new_params = [next(take) for _ in range(5)]
    if last:
        out_moments = [next(take) for _ in range(4)]
    else:
        new_moments = [next(take) for _ in range(5)]
    (wr, wall, we, na, sa, nb, sb, hpad, xcat, ypad, fb, hb, tc, dc, gt, gpad, gcat, zpad, db, gf) = take
    w_reduce, w_spatial, w_expand, gain, bias = mixed

    wr[...] = w_reduce[...].astype(BF16)
    for dy in range(3):
        for dx in range(3):
            tap = 3 * dy + dx
            wall[pl.ds(dx * 128, 128), pl.ds(dy * 128, 128)] = w_spatial[pl.ds(tap * 128, 128), :].astype(BF16)
    for q in range(4):
        we[:, pl.ds(q * 128, 128)] = w_expand[pl.ds(q, 128, stride=4), :].astype(BF16)
    gain_a, gain_b, gain_c = gain[:, 0:128], gain[:, 128:256], gain[:, 256:768]
    bias_a, bias_b, bias_c = bias[:, 0:128], bias[:, 128:256], bias[:, 256:768]

    hpad[0:8, :] = jnp.zeros((8, LANES), F32)
    hpad[PIXELS + 8 : PIXELS + 16, :] = jnp.zeros((8, LANES), F32)
    zpad[0:8, :] = jnp.zeros((8, 384), F32)
    zpad[PIXELS + 8 : PIXELS + 16, :] = jnp.zeros((8, 384), F32)
    ypad[0:PAD, :] = jnp.zeros((PAD, 384), F32)
    ypad[PIXELS + PAD : PIXELS + 2 * PAD, :] = jnp.zeros((PAD, 384), F32)
    gpad[0:PAD, :] = jnp.zeros((PAD, LANES), F32)
    gpad[PIXELS + PAD : PIXELS + 2 * PAD, :] = jnp.zeros((PAD, LANES), F32)
    column = lax.rem(lax.broadcasted_iota(jnp.int32, (ROWS, LANES), 0), WIDTH)
    has_left = column > 0
    has_right = column < WIDTH - 1

    first = db
    first[...] = contract(x_ref[...], wr[...], ((1,), (0,)))
    mean_a, scale_a = mean_and_scale(first, ROWS, CHUNKS, LANES)

    def forward_a(at, start, carry):
        normed = (first[at, :] - mean_a) * scale_a
        out = normed * gain_a + bias_a
        sigma = sigmoid(out)
        na[at, :] = normed
        sa[at, :] = sigma * (1.0 + out * (1.0 - sigma))
        hpad[pl.ds(pl.multiple_of(start + 8, 8), ROWS), :] = out * sigma
        return carry

    chunked(ROWS, CHUNKS, forward_a, 0)

    for c in range(CHUNKS):
        at, start = pl.ds(c * ROWS, ROWS), c * ROWS
        left = jnp.where(has_left, hpad[pl.ds(start + 7, ROWS), :], 0.0)
        right = jnp.where(has_right, hpad[pl.ds(start + 9, ROWS), :], 0.0)
        xcat[at, 0:128] = left.astype(BF16)
        xcat[at, 128:256] = hpad[pl.ds(start + 8, ROWS), :].astype(BF16)
        xcat[at, 256:384] = right.astype(BF16)

    ypad[pl.ds(PAD, PIXELS), :] = contract(xcat[...], wall[...], ((1,), (0,)))
    for c in range(CHUNKS):
        start = PAD + c * ROWS
        fb[pl.ds(c * ROWS, ROWS), :] = (
            ypad[pl.ds(start - WIDTH, ROWS), 0:128]
            + ypad[pl.ds(start, ROWS), 128:256]
            + ypad[pl.ds(start + WIDTH, ROWS), 256:384]
        )
    mean_b, scale_b = mean_and_scale(fb, ROWS, CHUNKS, LANES)

    def forward_b(at, start, carry):
        normed = (fb[at, :] - mean_b) * scale_b
        out = normed * gain_b + bias_b
        sigma = sigmoid(out)
        nb[at, :] = normed
        sb[at, :] = sigma * (1.0 + out * (1.0 - sigma))
        hb[at, :] = (out * sigma).astype(BF16)
        return carry

    chunked(ROWS, CHUNKS, forward_b, 0)

    tc[...] = contract(hb[...], we[...], ((1,), (0,)))
    mean_c, scale_c = mean_and_scale(tc, ROWS_C, CHUNKS_C, C_IN)
    zero_c = jnp.zeros((8, C_IN), F32)

    def backward_c(at, start, carry):
        sum_d, sum_dn = carry
        normed = (tc[at, :] - mean_c) * scale_c
        summed = normed * gain_c + bias_c + x_ref[at, :].astype(F32)
        sigma = sigmoid(summed)
        grad = cot_ref[at, :].astype(F32) * (sigma * (1.0 + summed * (1.0 - sigma)))
        tc[at, :] = normed
        dc[at, :] = grad
        return sum_d + rows_sum(grad), sum_dn + rows_sum(grad * normed)

    sums_c = chunked(ROWS_C, CHUNKS_C, backward_c, (zero_c, zero_c))
    dbias_c, dgain_c = total(sums_c[0]), total(sums_c[1])
    factor_c, mean_d, mean_dn = gain_c * scale_c, dbias_c * (1.0 / PIXELS), dgain_c * (1.0 / PIXELS)

    def third_c(at, start, carry):
        gt[at, :] = (factor_c * (dc[at, :] - mean_d - tc[at, :] * mean_dn)).astype(BF16)
        return carry

    chunked(ROWS_C, CHUNKS_C, third_c, 0)

    grad_expand = contract(hb[...], gt[...], ((0,), (0,)))

    def finish(index, at, grad, target_at=None):
        if last:
            moment = MOMENTUM * held[index][at] + grad
        else:
            moment = grad
        new_params[index][at] = mixed[index][at] - LEARN_RATE * moment
        return moment

    for q in range(4):
        at = (pl.ds(q, 128, stride=4), slice(None))
        moment = finish(2, at, grad_expand[:, q * 128 : (q + 1) * 128])
        if last:
            hpad[pl.ds(q, 128, stride=4), :] = moment
        else:
            new_moments[2][at] = moment
    if last:
        out_moments[2][...] = hpad[0:512, :].astype(BF16)

    db[...] = contract(gt[...], we[...], ((1,), (1,)))
    zero = jnp.zeros((8, LANES), F32)

    def grad_sums(source, slope, normed):
        def body(at, start, carry):
            sum_d, sum_dn = carry
            grad = source(at, start) * slope[at, :]
            db[at, :] = grad
            return sum_d + rows_sum(grad), sum_dn + rows_sum(grad * normed[at, :])

        sums = chunked(ROWS, CHUNKS, body, (zero, zero))
        return total(sums[0]), total(sums[1])

    dbias_b, dgain_b = grad_sums(lambda at, start: db[at, :], sb, nb)
    factor_b, mean_d, mean_dn = gain_b * scale_b, dbias_b * (1.0 / PIXELS), dgain_b * (1.0 / PIXELS)
    for c in range(CHUNKS):
        at = pl.ds(c * ROWS, ROWS)
        gpad[pl.ds(PAD + c * ROWS, ROWS), :] = factor_b * (db[at, :] - mean_d - nb[at, :] * mean_dn)
    for c in range(CHUNKS):
        at, start = pl.ds(c * ROWS, ROWS), PAD + c * ROWS
        gcat[at, 0:128] = gpad[pl.ds(start + WIDTH, ROWS), :].astype(BF16)
        gcat[at, 128:256] = gpad[pl.ds(start, ROWS), :].astype(BF16)
        gcat[at, 256:384] = gpad[pl.ds(start - WIDTH, ROWS), :].astype(BF16)

    zpad[pl.ds(8, PIXELS), :] = contract(gcat[...], wall[...], ((1,), (1,)))
    for c in range(CHUNKS):
        start = 8 + c * ROWS
        db[pl.ds(c * ROWS, ROWS), :] = (
            jnp.where(has_right, zpad[pl.ds(start + 1, ROWS), 0:128], 0.0)
            + zpad[pl.ds(start, ROWS), 128:256]
            + jnp.where(has_left, zpad[pl.ds(start - 1, ROWS), 256:384], 0.0)
        )
    dbias_a, dgain_a = grad_sums(lambda at, start: db[at, :], sa, na)
    factor_a, mean_d, mean_dn = gain_a * scale_a, dbias_a * (1.0 / PIXELS), dgain_a * (1.0 / PIXELS)

    def first_a(at, start, carry):
        gf[at, :] = (factor_a * (db[at, :] - mean_d - na[at, :] * mean_dn)).astype(BF16)
        return carry

    chunked(ROWS, CHUNKS, first_a, 0)

    grad_spatial = contract(xcat[...], gcat[...], ((0,), (0,)))
    for dy in range(3):
        for dx in range(3):
            at = (pl.ds((3 * dy + dx) * 128, 128), slice(None))
            moment = finish(1, at, grad_spatial[dx * 128 : (dx + 1) * 128, dy * 128 : (dy + 1) * 128])
            if last:
                out_moments[1][at] = moment.astype(BF16)
            else:
                new_moments[1][at] = moment

    grad_reduce = contract(gf[...], x_ref[...], ((0,), (0,)))
    for q in range(4):
        at = (pl.ds(q * 128, 128), slice(None))
        moment = finish(0, at, grad_reduce[:, q * 128 : (q + 1) * 128].T)
        if last:
            out_moments[0][at] = moment.astype(BF16)
        else:
            new_moments[0][at] = moment

    for index, grads in ((3, (dgain_a, dgain_b, dgain_c)), (4, (dbias_a, dbias_b, dbias_c))):
        for low, grad in zip((0, 128, 256), grads):
            at = (slice(None), slice(low, low + grad.shape[1]))
            moment = finish(index, at, grad)
            if last:
                base = (index - 3) * 768 + low
                out_moments[3][:, base : base + grad.shape[1]] = moment.astype(BF16)
            else:
                new_moments[index][at] = moment


def train_step(last, pixels, upstream, mixed, held):
    operands = (pixels, upstream) + tuple(mixed) + (tuple(held) if last else ())
    if last:
        outs = shaped(PARAMS, F32) + shaped(WEIGHTS + ((1, 1536),), BF16)
    else:
        outs = shaped(PARAMS, F32) * 2
    wide, thin = (PIXELS, C_IN), (PIXELS, LANES)
    scratch = [
        pltpu.VMEM((512, LANES), BF16),
        pltpu.VMEM((384, 384), BF16),
        pltpu.VMEM((LANES, 512), BF16),
        pltpu.VMEM(thin, F32),
        pltpu.VMEM(thin, F32),
        pltpu.VMEM(thin, F32),
        pltpu.VMEM(thin, F32),
        pltpu.VMEM((PIXELS + 16, LANES), F32),
        pltpu.VMEM((PIXELS, 384), BF16),
        pltpu.VMEM((PIXELS + 2 * PAD, 384), F32),
        pltpu.VMEM(thin, F32),
        pltpu.VMEM(thin, BF16),
        pltpu.VMEM(wide, F32),
        pltpu.VMEM(wide, F32),
        pltpu.VMEM(wide, BF16),
        pltpu.VMEM((PIXELS + 2 * PAD, LANES), F32),
        pltpu.VMEM((PIXELS, 384), BF16),
        pltpu.VMEM((PIXELS + 16, 384), F32),
        pltpu.VMEM(thin, F32),
        pltpu.VMEM(thin, BF16),
    ]
    return pl.pallas_call(
        functools.partial(step_kernel, last),
        out_shape=outs,
        in_specs=[VMEM] * len(operands),
        out_specs=(VMEM,) * len(outs),
        scratch_shapes=scratch,
        compiler_params=pltpu.CompilerParams(vmem_limit_bytes=40 * 2**20),
        name="last_step" if last else "first_step",
    )(*operands)


def average_kernel(*refs):
    reduce_ref, spatial_ref, expand_ref, gain, bias, out = refs[:6]
    (from_core, norm_core, sums_x, got_x, sums_y, got_y, sums_z, got_z, mine, other) = refs[6:16]
    core_send, core_recv, norm_send, norm_recv, x_send, x_recv, y_send, y_recv, z_send, z_recv, f_send, f_recv = refs[16:]
    me = lax.axis_index("dp")
    core = lax.rem(me, 2)
    z = lax.rem(lax.div(me, 2), 16)
    y = lax.rem(lax.div(me, 32), 4)
    x = lax.div(me, 128)
    twin = me + 1 - 2 * core

    def along_x(k):
        return me + (lax.rem(x + k, 4) - x) * 128

    def along_y(k):
        return me + (lax.rem(y + k, 4) - y) * 32

    def along_z(k):
        return me + (lax.rem(z + k, 16) - z) * 2

    barrier = pltpu.get_barrier_semaphore()
    peers = [along_z(8)]
    for k in (7, 9, 6, 10, 5, 11, 4, 12, 3, 13, 2, 14, 1, 15):
        peers.append(along_z(k))
    peers += [along_x(k) for k in (2, 1, 3)] + [along_y(k) for k in (2, 1, 3)] + [twin]
    for peer in peers:
        pl.semaphore_signal(barrier, inc=1, device_id=(peer,), device_id_type=MESH)
    pl.semaphore_wait(barrier, len(peers))

    def remote(src, dst, send, recv, peer):
        return pltpu.make_async_remote_copy(
            src_ref=src, dst_ref=dst, send_sem=send, recv_sem=recv, device_id=(peer,), device_id_type=MESH
        )

    def to_zero():
        return [
            remote(reduce_ref, from_core.at[pl.ds(0, 512)], core_send.at[0], core_recv.at[0], twin),
            remote(expand_ref, from_core.at[pl.ds(512, 512)], core_send.at[1], core_recv.at[1], twin),
            remote(gain, norm_core.at[0], norm_send.at[0], norm_recv.at[0], twin),
            remote(bias, norm_core.at[1], norm_send.at[1], norm_recv.at[1], twin),
        ]

    def to_one():
        return [
            remote(spatial_ref.at[pl.ds(0, 576)], from_core.at[pl.ds(0, 576)], core_send.at[0], core_recv.at[0], twin),
            remote(spatial_ref.at[pl.ds(576, 576)], from_core.at[pl.ds(576, 576)], core_send.at[1], core_recv.at[1], twin),
        ]

    @pl.when(core == 1)
    def _():
        for copy in to_zero():
            copy.start()
        arriving = to_one()
        for half in range(2):
            arriving[half].wait_recv()
            for k in (2 * half, 2 * half + 1):
                at = pl.ds(288 * k, 288)
                sums_x[k] = spatial_ref[at, :] + from_core[at, :]
        for copy in to_zero():
            copy.wait_send()

    @pl.when(core == 0)
    def _():
        for copy in to_one():
            copy.start()
        arriving = to_zero()
        arriving[0].wait_recv()
        for k in range(4):
            at = pl.ds(128 * k, 128)
            sums_x[k, 0:128, :] = reduce_ref[at, :] + from_core[at, :]
        arriving[1].wait_recv()
        for k in range(4):
            sums_x[k, 128:256, :] = expand_ref[pl.ds(128 * k, 128), :] + from_core[pl.ds(512 + 128 * k, 128), :]
        arriving[2].wait_recv()
        arriving[3].wait_recv()
        for k in range(4):
            source = (gain, bias)[k // 2]
            for t in range(3):
                low = ((k % 2) * 3 + t) * 128
                sums_x[k, 256 + t : 257 + t, :] = (
                    source[:, low : low + 128] + norm_core[k // 2, :, low : low + 128]
                )
            sums_x[k, 259:288, :] = jnp.zeros((29, LANES), F32)
        for copy in to_one():
            copy.wait_send()

    sends = []
    for k in (2, 1, 3):
        copy = remote(sums_x.at[lax.rem(x + k, 4)], got_x.at[k - 1], x_send.at[k - 1], x_recv.at[k - 1], along_x(k))
        copy.start()
        sends.append(copy)
    for copy in sends:
        copy.wait_recv()
    summed = sums_x[x] + got_x[0] + got_x[1] + got_x[2]

    @pl.when(core == 1)
    def _():
        for k in range(4):
            sums_y[k] = summed[72 * k : 72 * (k + 1)]

    @pl.when(core == 0)
    def _():
        for k in range(4):
            sums_y[k, 0:32, :] = summed[32 * k : 32 * (k + 1)]
            sums_y[k, 32:64, :] = summed[128 + 32 * k : 128 + 32 * (k + 1)]
            sums_y[k, 64:72, :] = summed[256:264]

    for copy in sends:
        copy.wait_send()

    sends = []
    for k in (2, 1, 3):
        copy = remote(sums_y.at[lax.rem(y + k, 4)], got_y.at[k - 1], y_send.at[k - 1], y_recv.at[k - 1], along_y(k))
        copy.start()
        sends.append(copy)
    for copy in sends:
        copy.wait_recv()
    got_y[3] = sums_y[y] + got_y[0] + got_y[1] + got_y[2]

    @pl.when(core == 1)
    def _():
        for k in range(8):
            sums_z[2 * k, 0:5, :] = got_y[3, 9 * k : 9 * k + 5, :]
            sums_z[2 * k, 5:8, :] = jnp.zeros((3, LANES), F32)
            sums_z[2 * k + 1, 0:5, :] = got_y[3, 9 * k + 4 : 9 * k + 9, :]
            sums_z[2 * k + 1, 5:8, :] = jnp.zeros((3, LANES), F32)

    @pl.when(core == 0)
    def _():
        for k in range(16):
            sums_z[k, 0:2, :] = got_y[3, 2 * k : 2 * k + 2, :]
            sums_z[k, 2:4, :] = got_y[3, 32 + 2 * k : 34 + 2 * k, :]
            sums_z[k, 4:8, :] = got_y[3, 64:68, :]

    for copy in sends:
        copy.wait_send()

    sends = []
    for k in (8, 7, 9, 6, 10, 5, 11, 4, 12, 3, 13, 2, 14, 1, 15):
        copy = remote(sums_z.at[lax.rem(z + k, 16)], got_z.at[k - 1], z_send.at[k - 1], z_recv.at[k - 1], along_z(k))
        copy.start()
        sends.append(copy)
    result = sums_z[z]
    for copy in reversed(sends):
        copy.wait_recv()
    for k in range(15):
        result = result + got_z[k]
    mine[...] = result * (1.0 / REPLICAS)
    copy = remote(mine, other, f_send, f_recv, twin)
    copy.start()
    for sent in sends:
        sent.wait_send()
    copy.wait_recv()

    @pl.when(core == 0)
    def _():
        out[0] = mine[...]
        out[1] = other[...]

    @pl.when(core == 1)
    def _():
        out[0] = other[...]
        out[1] = mine[...]

    copy.wait_send()


def averages(params):
    dma = pltpu.SemaphoreType.DMA
    found = pl.pallas_call(
        average_kernel,
        out_shape=jax.ShapeDtypeStruct((2, 8, LANES), F32),
        in_specs=[VMEM] * 5,
        out_specs=VMEM,
        scratch_shapes=[
            pltpu.VMEM((1152, LANES), F32),
            pltpu.VMEM((2, 1, 768), F32),
            pltpu.VMEM((4, 288, LANES), F32),
            pltpu.VMEM((3, 288, LANES), F32),
            pltpu.VMEM((4, 72, LANES), F32),
            pltpu.VMEM((4, 72, LANES), F32),
            pltpu.VMEM((16, 8, LANES), F32),
            pltpu.VMEM((15, 8, LANES), F32),
            pltpu.VMEM((8, LANES), F32),
            pltpu.VMEM((8, LANES), F32),
            dma((2,)), dma((2,)), dma((2,)), dma((2,)),
            dma((3,)), dma((3,)), dma((3,)), dma((3,)),
            dma((15,)), dma((15,)), dma, dma,
        ],
        compiler_params=pltpu.CompilerParams(collective_id=LEVELS, has_side_effects=True),
        name="averages",
    )(*params)
    me = lax.axis_index("dp")
    core, parity = me % 2, (me // 2) % 2
    avg_reduce = lax.dynamic_slice(found[0], (core, 0), (1, LANES)).reshape(LANES)
    avg_expand = lax.dynamic_slice(found[0], (2 + core, 0), (1, LANES)).reshape(LANES)
    avg_spatial = lax.dynamic_slice(found[1].reshape(-1), (parity * 64 + core * 288,), (288,))
    avg_norm = lax.dynamic_slice(found[0, 4:7].reshape(-1), (3 * (me % 128),), (3,))
    return avg_reduce, avg_spatial, avg_expand, avg_norm


def shards(images, cotangent, w_reduce, w_spatial, w_expand, norm_gain, norm_bias, round_index):
    params = (
        w_reduce.reshape(512, LANES),
        w_spatial.reshape(1152, LANES),
        w_expand.reshape(512, LANES),
        norm_gain,
        norm_bias,
    )
    bit = round_index[0] % LEVELS
    mixed = mix(bit, params)
    outs = train_step(False, images[0, 0], cotangent[0, 0], mixed, None)
    mixed = mix((round_index[0] + 1) % LEVELS, outs[:5])
    outs = train_step(True, images[1, 0], cotangent[1, 0], mixed, outs[5:])
    averaged = averages(outs[:5])
    momenta = tuple(member.reshape(1, -1) for member in outs[5:])
    return averaged + momenta


def solution(mesh):
    in_specs = (
        P(None, "dp", None, None),
        P(None, "dp", None, None),
        P("dp", None),
        P("dp", None),
        P("dp", None),
        P("dp", None),
        P("dp", None),
        P(),
    )
    out_specs = (P("dp"),) * 4 + (P("dp", None),) * 4
    return jax.shard_map(shards, mesh=mesh, in_specs=in_specs, out_specs=out_specs, check_vma=False)
```

```python
import functools

import jax
import jax.numpy as jnp
from jax import lax
from jax.experimental import pallas as pl
from jax.experimental.pallas import tpu as pltpu
from jax.sharding import PartitionSpec as P

LEARN_RATE = 0.01
MOMENTUM = 0.9
EPSILON = 1e-05

C_IN = 512
C_MID = 128
WIDTH = 28
PIXELS = 784
ROWS = 112
CHUNKS = PIXELS // ROWS
ROWS_C = 16
CHUNKS_C = PIXELS // ROWS_C
PAD = 32
LANES = 128
REPLICAS = 512
LEVELS = 9

F32 = jnp.float32
BF16 = jnp.bfloat16
MESH = pl.DeviceIdType.MESH
VMEM = pl.BlockSpec(memory_space=pltpu.VMEM)
HBM = pl.BlockSpec(memory_space=pltpu.HBM)
WEIGHTS = ((512, LANES), (1152, LANES), (512, LANES))
PARAMS = WEIGHTS + ((1, 768), (1, 768))
FLAT = ((1, 65536), (1, 147456), (1, 65536), (1, 1536))


def shaped(shapes, dtype):
    return tuple(jax.ShapeDtypeStruct(shape, dtype) for shape in shapes)


PIECES = ((0, 0, 512), (3, 0, 1), (4, 0, 1), (1, 0, 576), (1, 576, 576), (2, 0, 256), (2, 256, 256))


def gossip_kernel(bit, *refs):
    count = len(PARAMS)
    own, out = refs[:count], refs[count : 2 * count]
    held, theirs = refs[2 * count : 3 * count], refs[3 * count : 4 * count]
    send_sem, recv_sem, load_sem, store_sem = refs[4 * count :]
    me = lax.axis_index("dp")
    step = 1 << bit
    partner = me + step - 2 * step * lax.rem(lax.div(me, step), 2)
    loads = [pltpu.make_async_copy(own[k], held[k], load_sem.at[k]) for k in range(count)]
    barrier = pltpu.get_barrier_semaphore()
    pl.semaphore_signal(barrier, inc=1, device_id=(partner,), device_id_type=MESH)
    for k in (0, 3, 4, 1, 2):
        loads[k].start()
    pl.semaphore_wait(barrier, 1)
    copies = []
    for piece, (k, low, rows) in enumerate(PIECES):
        copy = pltpu.make_async_remote_copy(
            src_ref=own[k].at[pl.ds(low, rows)],
            dst_ref=theirs[k].at[pl.ds(low, rows)],
            send_sem=send_sem.at[piece],
            recv_sem=recv_sem.at[piece],
            device_id=(partner,),
            device_id_type=MESH,
        )
        copy.start()
        copies.append(copy)
    for load in loads:
        load.wait()
    stores = []
    for piece, (k, low, rows) in enumerate(PIECES):
        copies[piece].wait_recv()
        if rows == 1:
            held[k][...] = (held[k][...] + theirs[k][...]) * 0.5
        else:

            def body(index, carry):
                at = pl.ds(pl.multiple_of(low + index * 64, 64), 64)
                held[k][at, :] = (held[k][at, :] + theirs[k][at, :]) * 0.5
                return carry

            lax.fori_loop(0, rows // 64, body, 0)
        at = pl.ds(low, rows)
        store = pltpu.make_async_copy(held[k].at[at], out[k].at[at], store_sem.at[piece])
        store.start()
        stores.append(store)
    for copy in copies:
        copy.wait_send()
    for store in stores:
        store.wait()


def gossip(bit, *params):
    dma = pltpu.SemaphoreType.DMA
    return pl.pallas_call(
        functools.partial(gossip_kernel, bit),
        out_shape=shaped(PARAMS, F32),
        in_specs=[HBM] * 5,
        out_specs=(HBM,) * 5,
        scratch_shapes=[pltpu.VMEM(shape, F32) for shape in PARAMS * 2] + [dma((7,)), dma((7,)), dma((5,)), dma((7,))],
        compiler_params=pltpu.CompilerParams(collective_id=bit, has_side_effects=True),
        name=f"gossip{bit}",
    )(*params)


def mix(bit_choice, params):
    branches = [functools.partial(gossip, bit) for bit in range(LEVELS)]
    return lax.switch(bit_choice, branches, *params)


def contract(left, right, dims):
    return lax.dot_general(left, right, ((dims[0], dims[1]), ((), ())), preferred_element_type=F32)


def rows_sum(values):
    return jnp.sum(values.reshape(-1, 8, values.shape[-1]), axis=0)


def total(partial):
    return jnp.sum(partial, axis=0, keepdims=True)


def sigmoid(values):
    return 0.5 + 0.5 * jnp.tanh(0.5 * values)


def chunked(rows, chunks, body, init, unroll=1):
    def step(index, carry):
        return body(pl.ds(pl.multiple_of(index * rows, rows), rows), index * rows, carry)

    return lax.fori_loop(0, chunks, step, init, unroll=unroll)


def mean_and_scale(source, rows, chunks, width):
    zero = jnp.zeros((8, width), F32)
    mean = total(chunked(rows, chunks, lambda at, _, acc: acc + rows_sum(source[at, :]), zero)) * (1.0 / PIXELS)

    def spread(at, _, acc):
        center = source[at, :] - mean
        return acc + rows_sum(center * center)

    scale = lax.rsqrt(total(chunked(rows, chunks, spread, zero)) * (1.0 / PIXELS) + EPSILON)
    return mean, scale


def step_kernel(last, *refs):
    take = iter(refs)
    several = lambda count: [next(take) for _ in range(count)]
    images, cotangents = several(2)
    mixed_in = several(5)
    held_in = several(5) if last else []
    if last:
        out_moments = several(4)
        out_average = next(take)
    else:
        out_params, out_held = several(5), several(5)
    (wr, wall, we, na, sa, nb, sb, hpad, xcat, ypad, fb, hb, tc, dc, gt, gpad, gcat, zpad, db, gf) = several(20)
    x_ref, cot_ref = several(2)
    mixed, new_params, new_moments = several(5), several(5), several(5)
    held = several(5) if last else None
    flats = several(4) if last else None
    load_sem, store_sem = several(2)
    w_reduce, w_spatial, w_expand, gain, bias = mixed
    step_at = 1 if last else 0
    pairs = [
        (mixed_in[0], w_reduce),
        (images.at[step_at, 0], x_ref),
        (mixed_in[3], gain),
        (mixed_in[4], bias),
        (mixed_in[1], w_spatial),
        (mixed_in[2], w_expand),
        (cotangents.at[step_at, 0], cot_ref),
    ]
    if last:
        pairs += list(zip(held_in, held))
    loads = [pltpu.make_async_copy(src, dst, load_sem.at[k]) for k, (src, dst) in enumerate(pairs)]
    if last:
        sums = Sums(out_average, new_params, list(take))
        sums.greet()
    for load in loads:
        load.start()
    stores = []

    def store(src, dst):
        copy = pltpu.make_async_copy(src, dst, store_sem.at[len(stores)])
        copy.start()
        stores.append(copy)

    def store_pair(index):
        if not last:
            store(new_params[index], out_params[index])
            store(new_moments[index], out_held[index])

    loads[0].wait()
    wr[...] = w_reduce[...].astype(BF16)
    for load in loads[1:5]:
        load.wait()
    for dy in range(3):
        for dx in range(3):
            tap = 3 * dy + dx
            wall[pl.ds(dx * 128, 128), pl.ds(dy * 128, 128)] = w_spatial[pl.ds(tap * 128, 128), :].astype(BF16)
    loads[5].wait()
    for q in range(4):
        we[:, pl.ds(q * 128, 128)] = w_expand[pl.ds(q, 128, stride=4), :].astype(BF16)
    gain_a, gain_b, gain_c = gain[:, 0:128], gain[:, 128:256], gain[:, 256:768]
    bias_a, bias_b, bias_c = bias[:, 0:128], bias[:, 128:256], bias[:, 256:768]

    hpad[0:8, :] = jnp.zeros((8, LANES), F32)
    hpad[PIXELS + 8 : PIXELS + 16, :] = jnp.zeros((8, LANES), F32)
    zpad[0:8, :] = jnp.zeros((8, 384), F32)
    zpad[PIXELS + 8 : PIXELS + 16, :] = jnp.zeros((8, 384), F32)
    ypad[0:PAD, :] = jnp.zeros((PAD, 384), F32)
    ypad[PIXELS + PAD : PIXELS + 2 * PAD, :] = jnp.zeros((PAD, 384), F32)
    gpad[0:PAD, :] = jnp.zeros((PAD, LANES), F32)
    gpad[PIXELS + PAD : PIXELS + 2 * PAD, :] = jnp.zeros((PAD, LANES), F32)
    column = lax.rem(lax.broadcasted_iota(jnp.int32, (ROWS, LANES), 0), WIDTH)
    has_left = column > 0
    has_right = column < WIDTH - 1

    first = db
    first[...] = contract(x_ref[...], wr[...], ((1,), (0,)))
    mean_a, scale_a = mean_and_scale(first, ROWS, CHUNKS, LANES)

    def forward_a(at, start, carry):
        normed = (first[at, :] - mean_a) * scale_a
        out = normed * gain_a + bias_a
        sigma = sigmoid(out)
        na[at, :] = normed
        sa[at, :] = sigma * (1.0 + out * (1.0 - sigma))
        hpad[pl.ds(pl.multiple_of(start + 8, 8), ROWS), :] = out * sigma
        return carry

    chunked(ROWS, CHUNKS, forward_a, 0)

    for c in range(CHUNKS):
        at, start = pl.ds(c * ROWS, ROWS), c * ROWS
        left = jnp.where(has_left, hpad[pl.ds(start + 7, ROWS), :], 0.0)
        right = jnp.where(has_right, hpad[pl.ds(start + 9, ROWS), :], 0.0)
        xcat[at, 0:128] = left.astype(BF16)
        xcat[at, 128:256] = hpad[pl.ds(start + 8, ROWS), :].astype(BF16)
        xcat[at, 256:384] = right.astype(BF16)

    ypad[pl.ds(PAD, PIXELS), :] = contract(xcat[...], wall[...], ((1,), (0,)))
    for c in range(CHUNKS):
        start = PAD + c * ROWS
        fb[pl.ds(c * ROWS, ROWS), :] = (
            ypad[pl.ds(start - WIDTH, ROWS), 0:128]
            + ypad[pl.ds(start, ROWS), 128:256]
            + ypad[pl.ds(start + WIDTH, ROWS), 256:384]
        )
    mean_b, scale_b = mean_and_scale(fb, ROWS, CHUNKS, LANES)

    def forward_b(at, start, carry):
        normed = (fb[at, :] - mean_b) * scale_b
        out = normed * gain_b + bias_b
        sigma = sigmoid(out)
        nb[at, :] = normed
        sb[at, :] = sigma * (1.0 + out * (1.0 - sigma))
        hb[at, :] = (out * sigma).astype(BF16)
        return carry

    chunked(ROWS, CHUNKS, forward_b, 0)

    for load in loads[6:]:
        load.wait()
    tc[...] = contract(hb[...], we[...], ((1,), (0,)))
    mean_c, scale_c = mean_and_scale(tc, ROWS_C, CHUNKS_C, C_IN)
    zero_c = jnp.zeros((8, C_IN), F32)

    def backward_c(at, start, carry):
        sum_d, sum_dn = carry
        normed = (tc[at, :] - mean_c) * scale_c
        summed = normed * gain_c + bias_c + x_ref[at, :].astype(F32)
        sigma = sigmoid(summed)
        grad = cot_ref[at, :].astype(F32) * (sigma * (1.0 + summed * (1.0 - sigma)))
        tc[at, :] = normed
        dc[at, :] = grad
        return sum_d + rows_sum(grad), sum_dn + rows_sum(grad * normed)

    sums_c = chunked(ROWS_C, CHUNKS_C, backward_c, (zero_c, zero_c))
    dbias_c, dgain_c = total(sums_c[0]), total(sums_c[1])
    factor_c, mean_d, mean_dn = gain_c * scale_c, dbias_c * (1.0 / PIXELS), dgain_c * (1.0 / PIXELS)

    def third_c(at, start, carry):
        gt[at, :] = (factor_c * (dc[at, :] - mean_d - tc[at, :] * mean_dn)).astype(BF16)
        return carry

    chunked(ROWS_C, CHUNKS_C, third_c, 0)

    grad_expand = contract(hb[...], gt[...], ((0,), (0,)))

    def finish(index, at, grad, target_at=None):
        if last:
            moment = MOMENTUM * held[index][at] + grad
        else:
            moment = grad
        new_params[index][at] = mixed[index][at] - LEARN_RATE * moment
        return moment

    for q in range(4):
        at = (pl.ds(q, 128, stride=4), slice(None))
        new_moments[2][at] = finish(2, at, grad_expand[:, q * 128 : (q + 1) * 128])
    store_pair(2)
    if last:
        sums.meet()
        sums.send_expand()

    db[...] = contract(gt[...], we[...], ((1,), (1,)))
    zero = jnp.zeros((8, LANES), F32)

    def grad_sums(source, slope, normed):
        def body(at, start, carry):
            sum_d, sum_dn = carry
            grad = source(at, start) * slope[at, :]
            db[at, :] = grad
            return sum_d + rows_sum(grad), sum_dn + rows_sum(grad * normed[at, :])

        sums = chunked(ROWS, CHUNKS, body, (zero, zero))
        return total(sums[0]), total(sums[1])

    dbias_b, dgain_b = grad_sums(lambda at, start: db[at, :], sb, nb)
    factor_b, mean_d, mean_dn = gain_b * scale_b, dbias_b * (1.0 / PIXELS), dgain_b * (1.0 / PIXELS)
    for c in range(CHUNKS):
        at = pl.ds(c * ROWS, ROWS)
        gpad[pl.ds(PAD + c * ROWS, ROWS), :] = factor_b * (db[at, :] - mean_d - nb[at, :] * mean_dn)
    for c in range(CHUNKS):
        at, start = pl.ds(c * ROWS, ROWS), PAD + c * ROWS
        gcat[at, 0:128] = gpad[pl.ds(start + WIDTH, ROWS), :].astype(BF16)
        gcat[at, 128:256] = gpad[pl.ds(start, ROWS), :].astype(BF16)
        gcat[at, 256:384] = gpad[pl.ds(start - WIDTH, ROWS), :].astype(BF16)

    grad_spatial = contract(xcat[...], gcat[...], ((0,), (0,)))
    for dy in range(3):
        for dx in range(3):
            at = (pl.ds((3 * dy + dx) * 128, 128), slice(None))
            new_moments[1][at] = finish(1, at, grad_spatial[dx * 128 : (dx + 1) * 128, dy * 128 : (dy + 1) * 128])
    store_pair(1)
    if last:
        sums.send_spatial()
        sums.expand_along_x()

    zpad[pl.ds(8, PIXELS), :] = contract(gcat[...], wall[...], ((1,), (1,)))
    for c in range(CHUNKS):
        start = 8 + c * ROWS
        db[pl.ds(c * ROWS, ROWS), :] = (
            jnp.where(has_right, zpad[pl.ds(start + 1, ROWS), 0:128], 0.0)
            + zpad[pl.ds(start, ROWS), 128:256]
            + jnp.where(has_left, zpad[pl.ds(start - 1, ROWS), 256:384], 0.0)
        )
    dbias_a, dgain_a = grad_sums(lambda at, start: db[at, :], sa, na)
    factor_a, mean_d, mean_dn = gain_a * scale_a, dbias_a * (1.0 / PIXELS), dgain_a * (1.0 / PIXELS)

    def first_a(at, start, carry):
        gf[at, :] = (factor_a * (db[at, :] - mean_d - na[at, :] * mean_dn)).astype(BF16)
        return carry

    chunked(ROWS, CHUNKS, first_a, 0)

    if last:
        sums.spatial_along_x()
    grad_reduce = contract(gf[...], x_ref[...], ((0,), (0,)))
    for q in range(4):
        at = (pl.ds(q * 128, 128), slice(None))
        new_moments[0][at] = finish(0, at, grad_reduce[:, q * 128 : (q + 1) * 128].T)

    for index, grads in ((3, (dgain_a, dgain_b, dgain_c)), (4, (dbias_a, dbias_b, dbias_c))):
        for low, grad in zip((0, 128, 256), grads):
            at = (slice(None), slice(low, low + grad.shape[1]))
            new_moments[index][at] = finish(index, at, grad)
    store_pair(0)
    store_pair(3)
    store_pair(4)

    if last:
        sums.send_reduce()
        sums.reduce_along_x()
        for source, flat, out in zip(new_moments[:3], flats, out_moments):
            flatten(flat, source)
            store(flat, out)
        for k in range(2):
            flats[3][:, 768 * k : 768 * (k + 1)] = new_moments[3 + k][...].astype(BF16)
        store(flats[3], out_moments[3])
        sums.finish()
    for copy in stores:
        copy.wait()


def flatten(out, source):
    def body(index, carry):
        for s in range(8):
            row = index * 8 + s
            out[:, pl.ds(pl.multiple_of(row * LANES, LANES), LANES)] = source[pl.ds(row, 1), :].astype(BF16)
        return carry

    lax.fori_loop(0, source.shape[0] // 8, body, 0)


def train_step(last, images, cotangent, mixed, held):
    operands = (images, cotangent) + tuple(mixed) + (tuple(held) if last else ())
    if last:
        outs = shaped(FLAT, BF16) + shaped(((8, LANES),), F32)
        out_specs = (HBM,) * 4 + (VMEM,)
    else:
        outs = shaped(PARAMS, F32) * 2
        out_specs = (HBM,) * 10
    wide, thin = (PIXELS, C_IN), (PIXELS, LANES)
    scratch = [
        pltpu.VMEM((512, LANES), BF16),
        pltpu.VMEM((384, 384), BF16),
        pltpu.VMEM((LANES, 512), BF16),
        pltpu.VMEM(thin, F32),
        pltpu.VMEM(thin, F32),
        pltpu.VMEM(thin, F32),
        pltpu.VMEM(thin, F32),
        pltpu.VMEM((PIXELS + 16, LANES), F32),
        pltpu.VMEM((PIXELS, 384), BF16),
        pltpu.VMEM((PIXELS + 2 * PAD, 384), F32),
        pltpu.VMEM(thin, F32),
        pltpu.VMEM(thin, BF16),
        pltpu.VMEM(wide, F32),
        pltpu.VMEM(wide, F32),
        pltpu.VMEM(wide, BF16),
        pltpu.VMEM((PIXELS + 2 * PAD, LANES), F32),
        pltpu.VMEM((PIXELS, 384), BF16),
        pltpu.VMEM((PIXELS + 16, 384), F32),
        pltpu.VMEM(thin, F32),
        pltpu.VMEM(thin, BF16),
        pltpu.VMEM(wide, BF16),
        pltpu.VMEM(wide, BF16),
    ]
    scratch += [pltpu.VMEM(shape, F32) for shape in PARAMS * (4 if last else 3)]
    if last:
        scratch += [pltpu.VMEM(shape, BF16) for shape in FLAT]
    scratch += [pltpu.SemaphoreType.DMA((12,)), pltpu.SemaphoreType.DMA((10,))]
    if last:
        scratch += sums_scratch()
    params = pltpu.CompilerParams(vmem_limit_bytes=30 * 2**20)
    if last:
        params = pltpu.CompilerParams(vmem_limit_bytes=30 * 2**20, collective_id=LEVELS, has_side_effects=True)
    return pl.pallas_call(
        functools.partial(step_kernel, last),
        out_shape=outs,
        in_specs=[HBM] * len(operands),
        out_specs=out_specs,
        scratch_shapes=scratch,
        compiler_params=params,
        name="last_step" if last else "first_step",
    )(*operands)


def sums_scratch():
    dma = pltpu.SemaphoreType.DMA
    shapes = (
        (512, LANES),
        (1152, LANES),
        (512, LANES),
        (2, 1, 768),
        (4, 136, LANES),
        (3, 136, LANES),
        (4, 128, LANES),
        (3, 128, LANES),
        (4, 288, LANES),
        (3, 288, LANES),
        (4, 72, LANES),
        (4, 72, LANES),
        (16, 8, LANES),
        (15, 8, LANES),
        (8, LANES),
        (8, LANES),
        (8, LANES),
        (8, LANES),
    )
    sems = (6, 6, 3, 3, 3, 3, 3, 3, 3, 3, 15, 15, 1, 1)
    return [pltpu.VMEM(shape, F32) for shape in shapes] + [dma((count,)) for count in sems]


class Sums:
    def __init__(self, out, params, refs):
        self.out = out
        self.reduce, self.spatial, self.expand, self.gain, self.bias = params
        (self.twin_r, self.twin_s, self.twin_e, self.twin_n) = refs[0:4]
        (self.r_x, self.r_got, self.e_x, self.e_got, self.s_x, self.s_got) = refs[4:10]
        (self.sums_y, self.got_y, self.sums_z, self.got_z) = refs[10:14]
        (self.mine, self.other, self.flat, self.tall) = refs[14:18]
        (self.core_send, self.core_recv) = refs[18:20]
        (self.rx_send, self.rx_recv, self.ex_send, self.ex_recv, self.sx_send, self.sx_recv) = refs[20:26]
        (self.y_send, self.y_recv, self.z_send, self.z_recv, self.f_send, self.f_recv) = refs[26:32]
        me = lax.axis_index("dp")
        self.me = me
        self.core = lax.rem(me, 2)
        self.z = lax.rem(lax.div(me, 2), 16)
        self.y = lax.rem(lax.div(me, 32), 4)
        self.x = lax.div(me, 128)
        self.twin = me + 1 - 2 * self.core

    def along_x(self, k):
        return self.me + (lax.rem(self.x + k, 4) - self.x) * 128

    def along_y(self, k):
        return self.me + (lax.rem(self.y + k, 4) - self.y) * 32

    def along_z(self, k):
        return self.me + (lax.rem(self.z + k, 16) - self.z) * 2

    def peers(self):
        found = [self.along_z(k) for k in (8, 7, 9, 6, 10, 5, 11, 4, 12, 3, 13, 2, 14, 1, 15)]
        found += [self.along_x(k) for k in (2, 1, 3)] + [self.along_y(k) for k in (2, 1, 3)]
        return found + [self.twin]

    def greet(self):
        barrier = pltpu.get_barrier_semaphore()
        for peer in self.peers():
            pl.semaphore_signal(barrier, inc=1, device_id=(peer,), device_id_type=MESH)

    def meet(self):
        pl.semaphore_wait(pltpu.get_barrier_semaphore(), len(self.peers()))

    def remote(self, src, dst, send, recv, peer):
        return pltpu.make_async_remote_copy(
            src_ref=src, dst_ref=dst, send_sem=send, recv_sem=recv, device_id=(peer,), device_id_type=MESH
        )

    def to_twin(self, slot, src, dst):
        return self.remote(src, dst, self.core_send.at[slot], self.core_recv.at[slot], self.twin)

    def expand_copy(self):
        return self.to_twin(0, self.expand, self.twin_e)

    def reduce_copies(self):
        return [
            self.to_twin(1, self.reduce, self.twin_r),
            self.to_twin(2, self.gain, self.twin_n.at[0]),
            self.to_twin(3, self.bias, self.twin_n.at[1]),
        ]

    def spatial_copies(self):
        return [
            self.to_twin(4 + half, self.spatial.at[pl.ds(576 * half, 576)], self.twin_s.at[pl.ds(576 * half, 576)])
            for half in range(2)
        ]

    def x_copies(self, sums, got, send, recv):
        return [
            self.remote(
                sums.at[lax.rem(self.x + k, 4)], got.at[k - 1], send.at[k - 1], recv.at[k - 1], self.along_x(k)
            )
            for k in (2, 1, 3)
        ]

    def send_expand(self):
        @pl.when(self.core == 1)
        def _():
            self.expand_copy().start()

    def send_spatial(self):
        @pl.when(self.core == 0)
        def _():
            for copy in self.spatial_copies():
                copy.start()

    def send_reduce(self):
        @pl.when(self.core == 1)
        def _():
            for copy in self.reduce_copies():
                copy.start()

    def expand_along_x(self):
        @pl.when(self.core == 0)
        def _():
            self.expand_copy().wait_recv()
            for k in range(4):
                at = pl.ds(128 * k, 128)
                self.e_x[k] = self.expand[at, :] + self.twin_e[at, :]
            for copy in self.x_copies(self.e_x, self.e_got, self.ex_send, self.ex_recv):
                copy.start()

    def spatial_along_x(self):
        @pl.when(self.core == 1)
        def _():
            for half, copy in enumerate(self.spatial_copies()):
                copy.wait_recv()
                for k in (2 * half, 2 * half + 1):
                    at = pl.ds(288 * k, 288)
                    self.s_x[k] = self.spatial[at, :] + self.twin_s[at, :]
            for copy in self.x_copies(self.s_x, self.s_got, self.sx_send, self.sx_recv):
                copy.start()

    def reduce_along_x(self):
        @pl.when(self.core == 0)
        def _():
            for copy in self.reduce_copies():
                copy.wait_recv()
            for k in range(4):
                at = pl.ds(128 * k, 128)
                self.r_x[k, 0:128, :] = self.reduce[at, :] + self.twin_r[at, :]
                source = (self.gain, self.bias)[k // 2]
                for t in range(3):
                    low = ((k % 2) * 3 + t) * 128
                    self.r_x[k, 128 + t : 129 + t, :] = (
                        source[:, low : low + 128] + self.twin_n[k // 2, :, low : low + 128]
                    )
                self.r_x[k, 131:136, :] = jnp.zeros((5, LANES), F32)
            for copy in self.x_copies(self.r_x, self.r_got, self.rx_send, self.rx_recv):
                copy.start()

    def finish(self):
        def joined(sums, got, low, high):
            at = pl.ds(low, high - low)
            return sums[self.x, at, :] + got[0, at, :] + got[1, at, :] + got[2, at, :]

        @pl.when(self.core == 1)
        def _():
            for copy in self.x_copies(self.s_x, self.s_got, self.sx_send, self.sx_recv):
                copy.wait_recv()
            for k in range(4):
                self.sums_y[k] = joined(self.s_x, self.s_got, 72 * k, 72 * (k + 1))

        @pl.when(self.core == 0)
        def _():
            for copy in self.x_copies(self.e_x, self.e_got, self.ex_send, self.ex_recv):
                copy.wait_recv()
            for k in range(4):
                self.sums_y[k, 32:64, :] = joined(self.e_x, self.e_got, 32 * k, 32 * (k + 1))
            for copy in self.x_copies(self.r_x, self.r_got, self.rx_send, self.rx_recv):
                copy.wait_recv()
            norms = joined(self.r_x, self.r_got, 128, 136)
            for k in range(4):
                self.sums_y[k, 0:32, :] = joined(self.r_x, self.r_got, 32 * k, 32 * (k + 1))
                self.sums_y[k, 64:72, :] = norms

        y_sends = []
        for k in (2, 1, 3):
            copy = self.remote(
                self.sums_y.at[lax.rem(self.y + k, 4)],
                self.got_y.at[k - 1],
                self.y_send.at[k - 1],
                self.y_recv.at[k - 1],
                self.along_y(k),
            )
            copy.start()
            y_sends.append(copy)
        for copy in y_sends:
            copy.wait_recv()
        got_y, sums_z = self.got_y, self.sums_z
        got_y[3] = self.sums_y[self.y] + got_y[0] + got_y[1] + got_y[2]

        @pl.when(self.core == 1)
        def _():
            for k in range(8):
                sums_z[2 * k, 0:5, :] = got_y[3, 9 * k : 9 * k + 5, :]
                sums_z[2 * k, 5:8, :] = jnp.zeros((3, LANES), F32)
                sums_z[2 * k + 1, 0:5, :] = got_y[3, 9 * k + 4 : 9 * k + 9, :]
                sums_z[2 * k + 1, 5:8, :] = jnp.zeros((3, LANES), F32)

        @pl.when(self.core == 0)
        def _():
            for k in range(16):
                sums_z[k, 0:2, :] = got_y[3, 2 * k : 2 * k + 2, :]
                sums_z[k, 2:4, :] = got_y[3, 32 + 2 * k : 34 + 2 * k, :]
                sums_z[k, 4:8, :] = got_y[3, 64:68, :]

        z_sends = []
        for k in (8, 7, 9, 6, 10, 5, 11, 4, 12, 3, 13, 2, 14, 1, 15):
            copy = self.remote(
                sums_z.at[lax.rem(self.z + k, 16)],
                self.got_z.at[k - 1],
                self.z_send.at[k - 1],
                self.z_recv.at[k - 1],
                self.along_z(k),
            )
            copy.start()
            z_sends.append(copy)
        result = sums_z[self.z]
        for copy in reversed(z_sends):
            copy.wait_recv()
        for k in range(15):
            result = result + self.got_z[k]
        self.mine[...] = result * (1.0 / REPLICAS)
        last_copy = self.remote(self.mine, self.other, self.f_send.at[0], self.f_recv.at[0], self.twin)
        last_copy.start()

        @pl.when(self.core == 0)
        def _():
            for copy in self.spatial_copies():
                copy.wait_send()
            for copy in self.x_copies(self.e_x, self.e_got, self.ex_send, self.ex_recv):
                copy.wait_send()
            for copy in self.x_copies(self.r_x, self.r_got, self.rx_send, self.rx_recv):
                copy.wait_send()

        @pl.when(self.core == 1)
        def _():
            self.expand_copy().wait_send()
            for copy in self.reduce_copies():
                copy.wait_send()
            for copy in self.x_copies(self.s_x, self.s_got, self.sx_send, self.sx_recv):
                copy.wait_send()

        for copy in y_sends + z_sends:
            copy.wait_send()
        last_copy.wait_recv()

        @pl.when(self.core == 0)
        def _():
            self.flat[...] = self.mine[...]
            self.tall[...] = self.other[...]

        @pl.when(self.core == 1)
        def _():
            self.flat[...] = self.other[...]
            self.tall[...] = self.mine[...]

        last_copy.wait_send()
        self.publish()

    def publish(self):
        core, flat, tall, out = self.core, self.flat, self.tall, self.out
        lane = lax.broadcasted_iota(jnp.int32, (1, LANES), 1)

        def shifted(low, high, shift):
            back = lax.rem(LANES - shift, LANES)
            return jnp.where(lane < LANES - shift, pltpu.roll(low, back, 1), pltpu.roll(high, back, 1))

        out[0:1, :] = flat[pl.ds(core, 1), :]
        out[1:2, :] = flat[pl.ds(2 + core, 1), :]
        shift = 64 * lax.rem(self.z, 2) + 32 * core
        for t in range(3):
            out[2 + t : 3 + t, :] = shifted(
                tall[pl.ds(2 * core + t, 1), :], tall[pl.ds(2 * core + t + 1, 1), :], shift
            )
        at = 96 * self.y + 6 * self.z + 3 * core
        row = lax.div(at, LANES)
        out[5:6, :] = shifted(flat[pl.ds(4 + row, 1), :], flat[pl.ds(5 + row, 1), :], lax.rem(at, LANES))
        out[6:8, :] = jnp.zeros((2, LANES), F32)


def publish_kernel(*refs):
    sources, average, outs = refs[:4], refs[4], refs[5:9]
    avg_reduce, avg_spatial, avg_expand, avg_norm = refs[9:13]
    held, load_sem, store_sem = refs[13:17], refs[17], refs[18]
    loads = [pltpu.make_async_copy(sources[k], held[k], load_sem.at[k]) for k in range(4)]
    stores = [pltpu.make_async_copy(held[k], outs[k], store_sem.at[k]) for k in range(4)]
    for load in loads:
        load.start()
    avg_reduce[...] = average[0:1, :]
    avg_expand[...] = average[1:2, :]
    avg_spatial[:, 0:128] = average[2:3, :]
    avg_spatial[:, 128:256] = average[3:4, :]
    avg_spatial[:, 256:288] = average[4:5, 0:32]
    avg_norm[...] = average[5:6, 0:3]
    for load, store in zip(loads, stores):
        load.wait()
        store.start()
    for store in stores:
        store.wait()


def publish(moments, average):
    dma = pltpu.SemaphoreType.DMA
    return pl.pallas_call(
        publish_kernel,
        out_shape=shaped(FLAT, BF16) + shaped(((1, 128), (1, 288), (1, 128), (1, 3)), F32),
        in_specs=[HBM] * 4 + [VMEM],
        out_specs=(HBM,) * 4 + (VMEM,) * 4,
        scratch_shapes=[pltpu.VMEM(shape, BF16) for shape in FLAT] + [dma((4,)), dma((4,))],
        name="publish",
    )(*moments, average)


def shards(images, cotangent, w_reduce, w_spatial, w_expand, norm_gain, norm_bias, round_index):
    params = (
        w_reduce.reshape(512, LANES),
        w_spatial.reshape(1152, LANES),
        w_expand.reshape(512, LANES),
        norm_gain,
        norm_bias,
    )
    bit = round_index[0] % LEVELS
    mixed = mix(bit, params)
    outs = train_step(False, images, cotangent, mixed, None)
    mixed = mix((round_index[0] + 1) % LEVELS, outs[:5])
    *momenta, average = train_step(True, images, cotangent, mixed, outs[5:])
    outs = publish(momenta, average)
    return tuple(member[0] for member in outs[4:]) + tuple(outs[:4])


def solution(mesh):
    in_specs = (
        P(None, "dp", None, None),
        P(None, "dp", None, None),
        P("dp", None),
        P("dp", None),
        P("dp", None),
        P("dp", None),
        P("dp", None),
        P(),
    )
    out_specs = (P("dp"),) * 4 + (P("dp", None),) * 4
    return jax.shard_map(shards, mesh=mesh, in_specs=in_specs, out_specs=out_specs, check_vma=False)
```
